1024 devices in a mesh: section: 16 (over z_lo), dp: 16 (over x, y), head: 4 (over z_hi, core).
Axes of the slice: x: 4, y: 4, z: 32 (z_hi: 2, z_lo: 16; z = z_hi * 16 + z_lo), core: 2. Of those that a mesh axis runs over, the one named last changes fastest.
Arguments:
- segments: int32 [17, 2048], P(None, 'dp'), may hold values from 0 to 63, never falling along the last dimension, each value on 1 to 64 neighbouring positions
- section_input_stream: bfloat16 [16, 2048, 2048], P('section', 'dp', 'head'), may hold values from -16 to 16
- entering: bfloat16 [2048, 2048], P('dp'), may hold values from -16 to 16
- pending_first_values: bfloat16 [16, 2048, 512], P('section', 'dp', 'head'), may hold values from -6 to 6
- norm_gain_vector: float32 [16, 2048], P('section'), may hold values from 0.1 to 1.9
- query_weight: bfloat16 [16, 2048, 2048], P('section', None, 'head'), may hold values from -0.110485435 to 0.110485435
- key_weight: bfloat16 [16, 2048, 512], P('section', None, 'head'), may hold values from -0.110485435 to 0.110485435
- value_weight: bfloat16 [16, 2048, 512], P('section', None, 'head'), may hold values from -0.125 to 0.125
- output_weight: bfloat16 [16, 2048, 2048], P('section', None, 'head'), may hold values from -0.125 to 0.125
- query_key_scale: float32 [16, 16], P('section', 'head'), may hold values from 0.7 to 24
- value_blend_weight: float32 [16, 4], P('section', 'head'), may hold values from 0.3 to 1.5
- value_cotangent_rows: bfloat16 [16, 2, 2048, 512], P('section', None, 'dp', 'head'), may hold values from -0.125 to 0.125
Outputs:
- first_round: bfloat16 [16, 2048, 2048], P('section', 'dp', 'head')
- second_round: bfloat16 [16, 2048, 2048], P('section', 'dp', 'head')
- value_weight_grads: float32 [16, 2048, 512], P('section', 'dp', 'head')
The draws below stay inside these ranges and needn't reach their ends.
Inputs may be any that keep to these rules, and one draw needn't show every extreme that they name: `segments`: along each row document ids never fall, and a document holds at most half of 128 tokens.
All inputs are finite; a program needn't handle non-finite values.
Results may differ from the reference program's by a relative error of at most 0.018.
Values may be sent and summed in bfloat16 or wider, within the bound.
No kernel may reach another device: no remote copies, remote signals or barrier semaphores. Data moves between devices by JAX's collectives and lax.ppermute only.
A program may use at most 32 MiB of HBM per device.

```python
import math
import jax
import jax.numpy as jnp
import numpy as np
from jax import lax

D = 2048
HEADS = 16
KEY_VALUE_HEADS = 4
HEAD_WIDTH = 128
MB_TOK = 128
ROUNDS = 2
LAYER_COUNT = 16
TOKEN_COUNT = 2048
N_DP = 16


def stream_draw(key, array_shape):
    key_base = jax.random.fold_in(key, 0)
    values = jax.random.normal(key_base, array_shape, jnp.float32)
    return jnp.clip(values, -16.0, 16.0)


def draw_section_input_stream(key, part):
    return stream_draw(jax.random.fold_in(key, 3), (LAYER_COUNT, TOKEN_COUNT, D)).astype(jnp.bfloat16)


def draw_entering(key, part):
    return stream_draw(jax.random.fold_in(key, 5), (TOKEN_COUNT, D)).astype(jnp.bfloat16)


def query_key_pair(key):
    key_first, key_second = jax.random.split(jax.random.fold_in(key, 11))
    bound_value = 5.0 * D ** (-0.5)
    key_weights = jax.random.normal(key_first, (LAYER_COUNT, D, KEY_VALUE_HEADS * HEAD_WIDTH), jnp.float32) * D ** (-0.5)
    fresh_draw = jax.random.normal(key_second, (LAYER_COUNT, D, HEADS * HEAD_WIDTH), jnp.float32) * D ** (-0.5)
    query_weights = fresh_draw
    return (jnp.clip(query_weights, -bound_value, bound_value), jnp.clip(key_weights, -bound_value, bound_value))


def draw_query_weight(key, part):
    return query_key_pair(key)[0].astype(jnp.bfloat16)


def draw_key_weight(key, part):
    return query_key_pair(key)[1].astype(jnp.bfloat16)


def draw_query_key_scale(key, part):
    key_base = jax.random.fold_in(jax.random.fold_in(key, 17), 0)
    return jnp.exp(jax.random.uniform(key_base, (LAYER_COUNT, HEADS), jnp.float32, math.log(0.7), math.log(3.0)))


def block_levels(stream_key, extent, shards, least, high):
    def one(dim, blocks):
        heights = jax.random.uniform(jax.random.fold_in(jax.random.fold_in(stream_key, 6), dim), (blocks,), jnp.float32, least / len(shards), high / len(shards))
        return jnp.repeat(jnp.exp(heights), extent[dim] // blocks).reshape((-1,) + (1,) * (len(extent) - dim - 1))

    loudness = one(*shards[0])
    for cut in shards[1:]:
        loudness = loudness * one(*cut)
    return loudness


def split_up(amount, total, most, lean):
    weights = [(1 << 20) // math.isqrt(rank ** lean) + 1 for rank in range(2, amount + 1)]
    spare, given = total - most - (amount - 1), [1] * (amount - 1)
    while spare > 0:
        movable = [i for i in range(amount - 1) if given[i] < most]
        pool, left = sum([weights[i] for i in movable]), spare
        for i in movable:
            extra = min(most - given[i], max(1, left * weights[i] // pool), spare)
            given[i] = given[i] + extra
            spare = spare - extra
    return np.array([most] + given)


def ragged(rng, amount, total, reach, slope):
    if amount == 2:
        one = jax.random.randint(rng, (), max(1, total - reach), min(reach, total - 1) + 1)
        return jnp.stack([one, total - one])
    lengths = jnp.asarray(split_up(amount, total, reach, slope), jnp.int32)
    pairs = (amount - 1) // 2
    donor, receiver = lengths[1:1 + 2 * pairs:2], lengths[2:2 + 2 * pairs:2]
    margin = jnp.minimum(donor - 1, reach - receiver)
    passed = jax.random.randint(jax.random.fold_in(rng, 1), (pairs,), 0, 1 << 20) % (margin + 1)
    lengths = lengths.at[1:1 + 2 * pairs:2].set(donor - passed).at[2:2 + 2 * pairs:2].set(receiver + passed)
    return lengths[jax.random.permutation(jax.random.fold_in(rng, 2), amount)]


def bell_draw(key, extent, spread, bound, cuts=(), kind=jnp.bfloat16):
    entries = jax.random.normal(key, extent, jnp.float32) * spread
    if len(cuts) > 0:
        entries = block_levels(key, extent, cuts, -0.22, 0.18) * entries
    return jnp.clip(entries, min=-bound, max=bound).astype(kind)


def setup_inputs(seed: int = 0) -> dict:
    key_list = jax.random.split(jax.random.key(seed), 13)
    return {
        "segments": jax.vmap(lambda own: jnp.searchsorted(jnp.cumsum(ragged(own, 4 * N_DP, TOKEN_COUNT, MB_TOK // 2, 1)), jnp.arange(TOKEN_COUNT), side="right"))(jax.random.split(key_list[0], (LAYER_COUNT + 1))).reshape((LAYER_COUNT + 1, TOKEN_COUNT)).astype(jnp.int32),
        "section_input_stream": draw_section_input_stream(jax.random.fold_in(key_list[12], 71), 0),
        "entering": draw_entering(jax.random.fold_in(key_list[12], 71), 0),
        "pending_first_values": bell_draw(key_list[3], (LAYER_COUNT, TOKEN_COUNT, KEY_VALUE_HEADS * HEAD_WIDTH), 1.0, 6.0, ((0, 16), (1, 16), (2, 4))),
        "norm_gain_vector": jnp.clip(1.0 + 0.18 * jax.random.normal(key_list[4], (LAYER_COUNT, D), jnp.float32), 0.1, 1.9),
        "query_weight": draw_query_weight(jax.random.fold_in(key_list[12], 71), 0),
        "key_weight": draw_key_weight(jax.random.fold_in(key_list[12], 71), 0),
        "value_weight": bell_draw(key_list[7], (LAYER_COUNT, D, KEY_VALUE_HEADS * HEAD_WIDTH), D ** -0.5, 0.125, ((0, 16), (2, 4))),
        "output_weight": bell_draw(key_list[8], (LAYER_COUNT, HEADS * HEAD_WIDTH, D), (HEADS * HEAD_WIDTH) ** -0.5, 0.125, ((0, 16), (2, 4))),
        "query_key_scale": draw_query_key_scale(jax.random.fold_in(key_list[12], 71), 0),
        "value_blend_weight": jnp.clip(jnp.exp(math.log(1.5) - 1.60943787 * jax.random.uniform(key_list[10], (LAYER_COUNT, KEY_VALUE_HEADS), jnp.float32) ** block_levels(key_list[10], (LAYER_COUNT, KEY_VALUE_HEADS), ((0, 16), (1, 4)), -0.2, 0.2)), 0.3, 1.5),
        "value_cotangent_rows": bell_draw(key_list[11], (LAYER_COUNT, ROUNDS, TOKEN_COUNT, KEY_VALUE_HEADS * HEAD_WIDTH), 0.02, 0.125, ((0, 16), (2, 16), (3, 4))),
    }


epsilon = 1e-06

def rms_rows(values):
    return values * lax.rsqrt(lax.optimization_barrier(jnp.mean(values * values, axis=-1, keepdims=True)) + epsilon)

def block_layer(stream, segment_row, feature_gain, query_proj, key_proj, value_proj, out_proj, scales, mixing, earlier_values):
    tokens = stream.shape[0]
    stream_float = stream.astype(jnp.float32)
    normed = (rms_rows(stream_float) * feature_gain).astype(jnp.bfloat16)
    queries = jnp.dot(normed, query_proj, preferred_element_type=jnp.float32).reshape(tokens, HEADS, HEAD_WIDTH)
    key_rows = jnp.dot(normed, key_proj, preferred_element_type=jnp.float32).reshape(tokens, KEY_VALUE_HEADS, HEAD_WIDTH)
    values = jnp.dot(normed, value_proj, preferred_element_type=jnp.float32).reshape(tokens, KEY_VALUE_HEADS, HEAD_WIDTH)
    queries = rms_rows(queries)
    key_rows = rms_rows(key_rows)
    if earlier_values is None:
        mixed_values = values.astype(jnp.bfloat16)
        carried = mixed_values
    else:
        carried = earlier_values.reshape(tokens, KEY_VALUE_HEADS, HEAD_WIDTH)
        mixed_values = (values + mixing[None, :, None] * carried.astype(jnp.float32)).astype(jnp.bfloat16)
    group_size = HEADS // KEY_VALUE_HEADS
    queries = queries.reshape(N_DP, MB_TOK, KEY_VALUE_HEADS, group_size, HEAD_WIDTH)
    key_rows = key_rows.reshape(N_DP, MB_TOK, KEY_VALUE_HEADS, HEAD_WIDTH)
    mixed_blocks = mixed_values.reshape(N_DP, MB_TOK, KEY_VALUE_HEADS, HEAD_WIDTH)
    factor = (scales / math.sqrt(HEAD_WIDTH)).reshape(KEY_VALUE_HEADS, group_size)
    scores = jnp.einsum('nqkgd,ntkd->nkgqt', queries, key_rows) * factor[None, :, :, None, None]
    segment_blocks = segment_row.reshape(N_DP, MB_TOK)
    positions = jnp.arange(MB_TOK)
    allowed = (positions[:, None] >= positions[None, :])[None] & (segment_blocks[:, :, None] == segment_blocks[:, None, :])
    scores = jnp.where(allowed[:, None, None], scores, -jnp.inf)
    row_max = lax.optimization_barrier(jnp.max(scores, axis=-1, keepdims=True))
    exponent = jnp.exp(scores - row_max)
    weights = (exponent / lax.optimization_barrier(jnp.sum(exponent, axis=-1, keepdims=True))).astype(jnp.bfloat16)
    attended = jnp.einsum('nkgqt,ntkd->nqkgd', weights.astype(jnp.float32), mixed_blocks.astype(jnp.float32))
    attended = attended.astype(jnp.bfloat16).reshape(tokens, HEADS * HEAD_WIDTH)
    result = (stream_float + jnp.dot(attended, out_proj, preferred_element_type=jnp.float32)).astype(jnp.bfloat16)
    return (result, normed, carried.reshape(tokens, KEY_VALUE_HEADS * HEAD_WIDTH))

def reference(segments, section_input_stream, entering, pending_first_values, norm_gain_vector, query_weight, key_weight, value_weight, output_weight, query_key_scale, value_blend_weight, value_cotangent_rows):
    first_outputs = []
    first_normed = []
    first_carried = []
    for current_layer_index in range(LAYER_COUNT):
        earlier_values = None if current_layer_index == 0 else pending_first_values[current_layer_index]
        result, normed, carried = block_layer(section_input_stream[current_layer_index], segments[current_layer_index], norm_gain_vector[current_layer_index], query_weight[current_layer_index], key_weight[current_layer_index], value_weight[current_layer_index], output_weight[current_layer_index], query_key_scale[current_layer_index], value_blend_weight[current_layer_index], earlier_values)
        first_outputs.append(result)
        first_normed.append(normed)
        first_carried.append(carried)
    second_outputs = []
    gradients = []
    for current_layer_index in range(LAYER_COUNT):
        if current_layer_index == 0:
            stream = entering
            earlier_values = None
            segment_row = segments[LAYER_COUNT]
        else:
            stream = first_outputs[current_layer_index - 1]
            earlier_values = first_carried[current_layer_index - 1]
            segment_row = segments[current_layer_index - 1]
        result, normed, carried = block_layer(stream, segment_row, norm_gain_vector[current_layer_index], query_weight[current_layer_index], key_weight[current_layer_index], value_weight[current_layer_index], output_weight[current_layer_index], query_key_scale[current_layer_index], value_blend_weight[current_layer_index], earlier_values)
        second_outputs.append(result)
        gradient = jnp.dot(first_normed[current_layer_index].T, value_cotangent_rows[current_layer_index, 0], preferred_element_type=jnp.float32)
        gradient = gradient + jnp.dot(normed.T, value_cotangent_rows[current_layer_index, 1], preferred_element_type=jnp.float32)
        gradients.append(gradient)
    return (jnp.stack(first_outputs), jnp.stack(second_outputs), jnp.stack(gradients))
```

```python
import math

import jax
import jax.numpy as jnp
from jax import lax
from jax.sharding import PartitionSpec as P

D = 2048
HEAD_WIDTH = 128


epsilon = 1e-06


def passed_along(shard, axis, by):
    peers = lax.axis_size(axis)
    pairs = [(i, i + by) for i in range(peers) if 0 <= i + by < peers]
    return lax.ppermute(shard, axis, pairs)


def rms_rows(values):
    return values * lax.rsqrt(jnp.mean(values * values, axis=-1, keepdims=True) + epsilon)


def attend(
    full_rows,
    segment_row,
    feature_gain,
    query_proj,
    key_proj,
    value_proj,
    scales,
    mixing,
    earlier_values,
    is_first,
):
    tokens = full_rows.shape[0]
    local_heads = query_proj.shape[1] // HEAD_WIDTH
    local_kv = key_proj.shape[1] // HEAD_WIDTH
    group_size = local_heads // local_kv
    normed = (rms_rows(full_rows.astype(jnp.float32)) * feature_gain).astype(jnp.bfloat16)
    queries = jnp.dot(normed, query_proj, preferred_element_type=jnp.float32).reshape(
        tokens, local_kv, group_size, HEAD_WIDTH
    )
    key_rows = jnp.dot(normed, key_proj, preferred_element_type=jnp.float32).reshape(
        tokens, local_kv, HEAD_WIDTH
    )
    values = jnp.dot(normed, value_proj, preferred_element_type=jnp.float32)
    queries = rms_rows(queries)
    key_rows = rms_rows(key_rows)
    own_values = values.astype(jnp.bfloat16)
    blended = (
        values + jnp.repeat(mixing, HEAD_WIDTH)[None, :] * earlier_values.astype(jnp.float32)
    ).astype(jnp.bfloat16)
    mixed_values = jnp.where(is_first, own_values, blended)
    carried = jnp.where(is_first, own_values, earlier_values)
    factor = (scales / math.sqrt(HEAD_WIDTH)).reshape(local_kv, group_size)
    scores = jnp.einsum("qkgd,tkd->kgqt", queries, key_rows) * factor[:, :, None, None]
    positions = jnp.arange(tokens)
    allowed = (positions[:, None] >= positions[None, :]) & (
        segment_row[:, None] == segment_row[None, :]
    )
    scores = jnp.where(allowed, scores, -jnp.inf)
    row_max = jnp.max(scores, axis=-1, keepdims=True)
    exponent = jnp.exp(scores - row_max)
    weights = (exponent / jnp.sum(exponent, axis=-1, keepdims=True)).astype(jnp.bfloat16)
    attended = jnp.einsum(
        "kgqt,tkd->qkgd",
        weights,
        mixed_values.reshape(tokens, local_kv, HEAD_WIDTH),
        preferred_element_type=jnp.float32,
    )
    attended = attended.astype(jnp.bfloat16).reshape(tokens, local_heads * HEAD_WIDTH)
    return (attended, normed, carried)


def collect(piece):
    return lax.all_gather(piece, "head", axis=1, tiled=True)


def grad_term(normed_rows, cotangent):
    return jnp.einsum("td,tc->dc", normed_rows, cotangent, preferred_element_type=jnp.float32)


def per_device(
    segments,
    section_input_stream,
    entering,
    pending_first_values,
    norm_gain_vector,
    query_weight,
    key_weight,
    value_weight,
    output_weight,
    query_key_scale,
    value_blend_weight,
    value_cotangent_rows,
):
    section_index = lax.axis_index("section")
    head_index = lax.axis_index("head")
    is_first = section_index == 0
    shard_width = output_weight.shape[2]
    total_batches = segments.shape[0]
    grad_rows = D // lax.axis_size("dp")
    feature_gain = norm_gain_vector[0]
    query_proj = query_weight[0]
    key_proj = key_weight[0]
    value_proj = value_weight[0]
    out_proj = output_weight[0]
    scales = query_key_scale[0]
    mixing = value_blend_weight[0]

    def project(own_rows, attended):
        all_heads = collect(attended)
        return (
            own_rows.astype(jnp.float32)
            + jnp.dot(all_heads, out_proj, preferred_element_type=jnp.float32)
        ).astype(jnp.bfloat16)

    first_segments = lax.dynamic_index_in_dim(segments, section_index, 0, keepdims=False)
    own_first = section_input_stream[0]
    gathered_first = collect(own_first)
    attended_first, normed_first, carried_first = attend(
        gathered_first,
        first_segments,
        feature_gain,
        query_proj,
        key_proj,
        value_proj,
        scales,
        mixing,
        pending_first_values[0],
        is_first,
    )
    output_first = project(own_first, attended_first)
    received_own, received_values = passed_along((output_first, carried_first), "section", 1)
    entering_own = lax.dynamic_slice_in_dim(entering, head_index * shard_width, shard_width, 1)
    own_second = jnp.where(is_first, entering_own, received_own)
    gathered_second = collect(own_second)
    second_index = (section_index + total_batches - 1) % total_batches
    second_segments = lax.dynamic_index_in_dim(segments, second_index, 0, keepdims=False)
    attended_second, normed_second, carried_second = attend(
        gathered_second,
        second_segments,
        feature_gain,
        query_proj,
        key_proj,
        value_proj,
        scales,
        mixing,
        received_values,
        is_first,
    )
    output_second = project(own_second, attended_second)
    first_term = grad_term(normed_first, value_cotangent_rows[0, 0])
    second_term = grad_term(normed_second, value_cotangent_rows[0, 1])
    partial = first_term + second_term
    replicas = lax.axis_size("dp")
    pieces = partial.astype(jnp.bfloat16).reshape(replicas, grad_rows, partial.shape[1])
    exchanged = lax.all_to_all(pieces, "dp", 0, 0, tiled=True)
    gradients = jnp.sum(exchanged.astype(jnp.float32), axis=0)
    return (output_first[None], output_second[None], gradients[None])


def solution(mesh):
    return jax.shard_map(
        per_device,
        mesh=mesh,
        in_specs=(
            P(None, "dp"),
            P("section", "dp", "head"),
            P("dp", None),
            P("section", "dp", "head"),
            P("section", None),
            P("section", None, "head"),
            P("section", None, "head"),
            P("section", None, "head"),
            P("section", None, "head"),
            P("section", "head"),
            P("section", "head"),
            P("section", None, "dp", "head"),
        ),
        out_specs=(
            P("section", "dp", "head"),
            P("section", "dp", "head"),
            P("section", "dp", "head"),
        ),
        check_vma=False,
    )
```

```python
import math

import jax
import jax.numpy as jnp
from jax import lax
from jax.experimental import pallas as pl
from jax.experimental.pallas import tpu as pltpu
from jax.sharding import PartitionSpec as P

HEAD_WIDTH = 128
EPSILON = 1e-06
LANES = 128

VMEM = pl.BlockSpec(memory_space=pltpu.VMEM)
SMEM = pl.BlockSpec(memory_space=pltpu.SMEM)
HBM = pl.BlockSpec(memory_space=pltpu.HBM)


def collect(piece):
    return lax.all_gather(piece, "head", axis=1, tiled=True)


def collect_chip(piece):
    peers = lax.axis_size("head")
    chips = [[i, i + 1] for i in range(0, peers, 2)]
    return lax.all_gather(piece, "head", axis_index_groups=chips)


def collect_planes(piece):
    peers = lax.axis_size("head")
    pairs = [[i, i + peers // 2] for i in range(peers // 2)]
    return lax.all_gather(piece, "head", axis_index_groups=pairs)


def next_section(piece):
    peers = lax.axis_size("section")
    return lax.ppermute(piece, "section", [(i, i + 1) for i in range(peers - 1)])


def rms_rows(values):
    return values * lax.rsqrt(jnp.mean(values * values, axis=-1, keepdims=True) + EPSILON)


def begin(pairs, semaphores):
    copies = [pltpu.make_async_copy(src, dst, semaphores.at[i]) for i, (src, dst) in enumerate(pairs)]
    for copy in copies:
        copy.start()
    return copies


def root_mean_square(x_ref):
    tokens, width = x_ref.shape
    squares = jnp.zeros((tokens, LANES), jnp.float32)
    for start in range(0, width, LANES):
        part = x_ref[:, start : start + LANES].astype(jnp.float32)
        squares += part * part
    return lax.rsqrt(jnp.sum(squares, axis=-1, keepdims=True) / width + EPSILON)


def normalise(x_ref, root, gain_ref, normed_ref):
    for start in range(0, x_ref.shape[1], LANES):
        columns = slice(start, start + LANES)
        part = x_ref[:, columns].astype(jnp.float32)
        normed_ref[:, columns] = (part * root * gain_ref[:, columns]).astype(jnp.bfloat16)


def attend(
    normed_ref, row, is_first, key_ref, value_ref, query_ref, scale_ref, blend_ref, earlier_ref, waits, attended_ref,
    carried_ref,
):
    key_wait, value_wait, earlier_wait, query_wait = waits
    tokens = normed_ref.shape[0]
    local_heads = query_ref.shape[1] // HEAD_WIDTH
    across = jnp.broadcast_to(row, (tokens, tokens))
    down = across.T
    later = lax.broadcasted_iota(jnp.int32, (tokens, tokens), 0)
    sooner = lax.broadcasted_iota(jnp.int32, (tokens, tokens), 1)
    allowed = (later >= sooner) & (across == down)
    normed = normed_ref[...]
    key_wait()
    keys = rms_rows(jnp.dot(normed, key_ref[...], preferred_element_type=jnp.float32))
    value_wait()
    values = jnp.dot(normed, value_ref[...], preferred_element_type=jnp.float32)
    earlier_wait()
    own = values.astype(jnp.bfloat16)
    earlier = earlier_ref[...]
    blended = (values + blend_ref[0, 0] * earlier.astype(jnp.float32)).astype(jnp.bfloat16)
    mixed = jnp.where(is_first, own, blended)
    if carried_ref is not None:
        carried_ref[...] = jnp.where(is_first, own, earlier)
    query_wait()
    queries = jnp.dot(normed, query_ref[...], preferred_element_type=jnp.float32)
    for head in range(local_heads):
        columns = slice(head * HEAD_WIDTH, (head + 1) * HEAD_WIDTH)
        query = rms_rows(queries[:, columns])
        scores = lax.dot_general(
            query,
            keys,
            (((1,), (1,)), ((), ())),
            precision=lax.Precision.HIGHEST,
            preferred_element_type=jnp.float32,
        )
        scores = scores * (scale_ref[0, head] / math.sqrt(HEAD_WIDTH))
        scores = jnp.where(allowed, scores, -jnp.inf)
        exponent = jnp.exp(scores - jnp.max(scores, axis=-1, keepdims=True))
        weights = (exponent / jnp.sum(exponent, axis=-1, keepdims=True)).astype(jnp.bfloat16)
        attended_ref[:, columns] = jnp.dot(
            weights, mixed, preferred_element_type=jnp.float32
        ).astype(jnp.bfloat16)


def first_kernel(
    where_ref, scale_ref, blend_ref, x_ref, segments_in, gain_in, earlier_in, key_in, value_in, query_in,
    attended_ref, carried_ref, normed_out,
    segments_ref, gain_ref, earlier_ref, key_ref, value_ref, query_ref, normed_ref, semaphores,
):
    gain, segments, key, value, earlier, query = begin(
        [
            (gain_in, gain_ref),
            (segments_in, segments_ref),
            (key_in, key_ref),
            (value_in, value_ref),
            (earlier_in, earlier_ref),
            (query_in, query_ref),
        ],
        semaphores,
    )
    root = root_mean_square(x_ref)
    gain.wait()
    normalise(x_ref, root, gain_ref, normed_ref)
    normed_copy = pltpu.make_async_copy(normed_ref, normed_out, semaphores.at[6])
    normed_copy.start()
    segments.wait()
    row = segments_ref[pl.ds(where_ref[0], 1), :]
    attend(
        normed_ref, row, where_ref[0] == 0, key_ref, value_ref, query_ref, scale_ref, blend_ref, earlier_ref,
        (key.wait, value.wait, earlier.wait, query.wait), attended_ref, carried_ref,
    )
    normed_copy.wait()


def second_kernel(
    where_ref, scale_ref, blend_ref, received_ref, entering_ref, segments_ref, gain_ref, earlier_ref, key_ref,
    value_ref, query_ref,
    attended_ref, own_ref, normed_ref,
    x_ref,
):
    is_first = where_ref[0] == 0
    shard = own_ref.shape[1]
    cores, planes = received_ref.shape[:2]

    @pl.when(is_first)
    def _():
        x_ref[...] = entering_ref[...]

    @pl.when(jnp.logical_not(is_first))
    def _():
        for core in range(cores):
            for plane in range(planes):
                head = plane * cores + core
                x_ref[:, head * shard : (head + 1) * shard] = received_ref[core, plane]

    for head in range(cores * planes):

        @pl.when(where_ref[3] == head)
        def _():
            own_ref[...] = x_ref[:, head * shard : (head + 1) * shard]

    normalise(x_ref, root_mean_square(x_ref), gain_ref, normed_ref)
    row = segments_ref[pl.ds(where_ref[1], 1), :]
    ready = (lambda: None,) * 4
    attend(
        normed_ref, row, is_first, key_ref, value_ref, query_ref, scale_ref, blend_ref, earlier_ref, ready,
        attended_ref, None,
    )


def pieces_kernel(before_ref, normed_ref, cotangent_ref, pieces_ref):
    replicas = pieces_ref.shape[0]
    rows = normed_ref.shape[1] // replicas
    contract = (((1,), (0,)), ((), ()))
    first = cotangent_ref[0].astype(jnp.float32).T.astype(jnp.bfloat16)
    second = cotangent_ref[1].astype(jnp.float32).T.astype(jnp.bfloat16)
    for replica in range(replicas):
        columns = slice(replica * rows, (replica + 1) * rows)
        term = lax.dot_general(first, before_ref[:, columns], contract, preferred_element_type=jnp.float32)
        term += lax.dot_general(second, normed_ref[:, columns], contract, preferred_element_type=jnp.float32)
        pieces_ref[replica] = term.astype(jnp.bfloat16)


def total_kernel(pieces_ref, total_ref):
    total = pieces_ref[0].astype(jnp.float32)
    for replica in range(1, pieces_ref.shape[0]):
        total += pieces_ref[replica].astype(jnp.float32)
    total_ref[...] = total.T


PARAMS = pltpu.CompilerParams(vmem_limit_bytes=16 * 1024 * 1024)


def per_device(
    segments,
    section_input_stream,
    entering,
    pending_first_values,
    norm_gain_vector,
    query_weight,
    key_weight,
    value_weight,
    output_weight,
    query_key_scale,
    value_blend_weight,
    value_cotangent_rows,
):
    section_index = lax.axis_index("section")
    head_index = lax.axis_index("head")
    is_first = section_index == 0
    width = output_weight.shape[1]
    shard_width = output_weight.shape[2]
    total_batches, tokens = segments.shape
    kv_width = key_weight.shape[2]
    replicas = lax.axis_size("dp")
    grad_rows = width // replicas
    query_proj = query_weight[0]
    key_proj = key_weight[0]
    value_proj = value_weight[0]
    out_proj = output_weight[0]
    q_width = query_proj.shape[1]
    shape = jax.ShapeDtypeStruct
    half, floats = jnp.bfloat16, jnp.float32
    slots = jnp.arange(4, dtype=jnp.int32)
    before = jnp.where(is_first, total_batches - 1, section_index - 1)
    plane = head_index // (lax.axis_size("head") // 2)
    where = jnp.where(
        slots < 2,
        jnp.where(slots == 0, section_index, before),
        jnp.where(slots == 2, plane, head_index),
    ).astype(jnp.int32)
    own_first = section_input_stream[0]

    def project(own_rows, attended):
        return (
            own_rows.astype(floats)
            + jnp.dot(collect(attended), out_proj, preferred_element_type=floats)
        ).astype(half)

    in_hbm = [
        pltpu.with_memory_space_constraint(array, pltpu.HBM)
        for array in (segments, norm_gain_vector, pending_first_values[0], key_proj, value_proj, query_proj)
    ]
    attended_first, carried_first, normed_first = pl.pallas_call(
        first_kernel,
        out_shape=(
            shape((tokens, q_width), half),
            shape((tokens, kv_width), half),
            shape((tokens, width), half),
        ),
        in_specs=[SMEM] * 3 + [VMEM] + [HBM] * 6,
        out_specs=(VMEM, VMEM, HBM),
        scratch_shapes=[pltpu.VMEM(array.shape, array.dtype) for array in in_hbm]
        + [pltpu.VMEM((tokens, width), half), pltpu.SemaphoreType.DMA((7,))],
        compiler_params=PARAMS,
        name="first_round",
    )(where, query_key_scale, value_blend_weight, collect(own_first), *in_hbm)
    output_first = project(own_first, attended_first)
    received_half = next_section(collect_planes(output_first))
    received_values = next_section(carried_first)
    attended_second, own_second, normed_second = pl.pallas_call(
        second_kernel,
        out_shape=(
            shape((tokens, q_width), half),
            shape((tokens, shard_width), half),
            shape((tokens, width), half),
        ),
        in_specs=[SMEM] * 3 + [VMEM] * 8,
        out_specs=(VMEM,) * 3,
        scratch_shapes=[pltpu.VMEM((tokens, width), half)],
        compiler_params=PARAMS,
        name="second_round",
    )(
        where, query_key_scale, value_blend_weight, collect_chip(received_half), entering, segments, norm_gain_vector,
        received_values, key_proj, value_proj, query_proj,
    )
    pieces = pl.pallas_call(
        pieces_kernel,
        out_shape=shape((replicas, kv_width, grad_rows), half),
        in_specs=[VMEM] * 3,
        out_specs=VMEM,
        compiler_params=PARAMS,
        name="pieces",
    )(normed_first, normed_second, value_cotangent_rows[0])
    exchanged = lax.all_to_all(pieces, "dp", 0, 0, tiled=True)
    output_second = project(own_second, attended_second)
    gradients = pl.pallas_call(
        total_kernel,
        out_shape=shape((grad_rows, kv_width), floats),
        in_specs=[VMEM],
        out_specs=VMEM,
        compiler_params=PARAMS,
        name="gradient_total",
    )(exchanged)
    return (output_first[None], output_second[None], gradients[None])


def solution(mesh):
    return jax.shard_map(
        per_device,
        mesh=mesh,
        in_specs=(
            P(None, "dp"),
            P("section", "dp", "head"),
            P("dp", None),
            P("section", "dp", "head"),
            P("section", None),
            P("section", None, "head"),
            P("section", None, "head"),
            P("section", None, "head"),
            P("section", None, "head"),
            P("section", "head"),
            P("section", "head"),
            P("section", None, "dp", "head"),
        ),
        out_specs=(
            P("section", "dp", "head"),
            P("section", "dp", "head"),
            P("section", "dp", "head"),
        ),
        check_vma=False,
    )
```

```python
import math

import jax
import jax.numpy as jnp
from jax import lax
from jax.experimental import pallas as pl
from jax.experimental.pallas import tpu as pltpu
from jax.sharding import PartitionSpec as P

HEAD_WIDTH = 128
EPSILON = 1e-06
LANES = 128

VMEM = pl.BlockSpec(memory_space=pltpu.VMEM)
SMEM = pl.BlockSpec(memory_space=pltpu.SMEM)
HBM = pl.BlockSpec(memory_space=pltpu.HBM)


def collect(piece):
    return lax.all_gather(piece, "head", axis=1, tiled=True)


def collect_chip(piece):
    peers = lax.axis_size("head")
    chips = [[i, i + 1] for i in range(0, peers, 2)]
    return lax.all_gather(piece, "head", axis_index_groups=chips)


def collect_planes(piece):
    peers = lax.axis_size("head")
    pairs = [[i, i + peers // 2] for i in range(peers // 2)]
    return lax.all_gather(piece, "head", axis_index_groups=pairs)


def swap_planes(piece):
    peers = lax.axis_size("head")
    return lax.ppermute(piece, "head", [(i, (i + peers // 2) % peers) for i in range(peers)])


def next_section(piece):
    peers = lax.axis_size("section")
    return lax.ppermute(piece, "section", [(i, i + 1) for i in range(peers - 1)])


def rms_rows(values):
    return values * lax.rsqrt(jnp.mean(values * values, axis=-1, keepdims=True) + EPSILON)


def begin(pairs, semaphores):
    copies = [pltpu.make_async_copy(src, dst, semaphores.at[i]) for i, (src, dst) in enumerate(pairs)]
    for copy in copies:
        copy.start()
    return copies


def root_mean_square(x_ref):
    tokens, width = x_ref.shape
    squares = jnp.zeros((tokens, LANES), jnp.float32)
    for start in range(0, width, LANES):
        part = x_ref[:, start : start + LANES].astype(jnp.float32)
        squares += part * part
    return lax.rsqrt(jnp.sum(squares, axis=-1, keepdims=True) / width + EPSILON)


def normalise(x_ref, root, gain_ref, normed_ref):
    for start in range(0, x_ref.shape[1], LANES):
        columns = slice(start, start + LANES)
        part = x_ref[:, columns].astype(jnp.float32)
        normed_ref[:, columns] = (part * root * gain_ref[:, columns]).astype(jnp.bfloat16)


def attend(
    normed_ref, row, is_first, key_ref, value_ref, query_ref, scale_ref, blend_ref, earlier_ref, waits, attended_ref,
    carried_ref,
):
    key_wait, value_wait, earlier_wait, query_wait = waits
    tokens = normed_ref.shape[0]
    local_heads = query_ref.shape[1] // HEAD_WIDTH
    across = jnp.broadcast_to(row, (tokens, tokens))
    down = across.T
    later = lax.broadcasted_iota(jnp.int32, (tokens, tokens), 0)
    sooner = lax.broadcasted_iota(jnp.int32, (tokens, tokens), 1)
    allowed = (later >= sooner) & (across == down)
    normed = normed_ref[...]
    key_wait()
    keys = rms_rows(jnp.dot(normed, key_ref[...], preferred_element_type=jnp.float32))
    value_wait()
    values = jnp.dot(normed, value_ref[...], preferred_element_type=jnp.float32)
    earlier_wait()
    own = values.astype(jnp.bfloat16)
    earlier = earlier_ref[...]
    blended = (values + blend_ref[0, 0] * earlier.astype(jnp.float32)).astype(jnp.bfloat16)
    mixed = jnp.where(is_first, own, blended)
    if carried_ref is not None:
        carried_ref[...] = jnp.where(is_first, own, earlier)
    query_wait()
    queries = jnp.dot(normed, query_ref[...], preferred_element_type=jnp.float32)
    for head in range(local_heads):
        columns = slice(head * HEAD_WIDTH, (head + 1) * HEAD_WIDTH)
        query = rms_rows(queries[:, columns])
        scores = lax.dot_general(
            query,
            keys,
            (((1,), (1,)), ((), ())),
            precision=lax.Precision.HIGHEST,
            preferred_element_type=jnp.float32,
        )
        scores = scores * (scale_ref[0, head] / math.sqrt(HEAD_WIDTH))
        scores = jnp.where(allowed, scores, -jnp.inf)
        exponent = jnp.exp(scores - jnp.max(scores, axis=-1, keepdims=True))
        weights = (exponent / jnp.sum(exponent, axis=-1, keepdims=True)).astype(jnp.bfloat16)
        attended_ref[:, columns] = jnp.dot(
            weights, mixed, preferred_element_type=jnp.float32
        ).astype(jnp.bfloat16)


def first_kernel(
    where_ref, blend_ref, x_ref, segments_in, gain_in, scale_in, earlier_in, key_in, value_in, query_in,
    attended_ref, carried_ref, normed_out,
    segments_ref, gain_ref, scale_ref, earlier_ref, key_ref, value_ref, query_ref, normed_ref, semaphores,
):
    gain, segments, scale, earlier, key, value, query = begin(
        [
            (gain_in, gain_ref),
            (segments_in, segments_ref),
            (scale_in, scale_ref),
            (earlier_in, earlier_ref),
            (key_in, key_ref),
            (value_in, value_ref),
            (query_in, query_ref),
        ],
        semaphores,
    )
    root = root_mean_square(x_ref)
    gain.wait()
    normalise(x_ref, root, gain_ref, normed_ref)
    normed_copy = pltpu.make_async_copy(normed_ref, normed_out, semaphores.at[7])
    normed_copy.start()
    segments.wait()
    scale.wait()
    row = segments_ref[pl.ds(where_ref[0], 1), :]
    attend(
        normed_ref, row, where_ref[0] == 0, key_ref, value_ref, query_ref, scale_ref, blend_ref, earlier_ref,
        (key.wait, value.wait, earlier.wait, query.wait), attended_ref, carried_ref,
    )
    normed_copy.wait()


def gradient_pieces(before_ref, normed_ref, cotangent_ref, pieces_ref):
    replicas = pieces_ref.shape[0]
    rows = normed_ref.shape[1] // replicas
    contract = (((1,), (0,)), ((), ()))
    first = cotangent_ref[0].astype(jnp.float32).T.astype(jnp.bfloat16)
    second = cotangent_ref[1].astype(jnp.float32).T.astype(jnp.bfloat16)
    for replica in range(replicas):
        columns = slice(replica * rows, (replica + 1) * rows)
        term = lax.dot_general(first, before_ref[:, columns], contract, preferred_element_type=jnp.float32)
        term += lax.dot_general(second, normed_ref[:, columns], contract, preferred_element_type=jnp.float32)
        pieces_ref[replica] = term.astype(jnp.bfloat16)


def second_kernel(
    where_ref, blend_ref, scale_in, received_ref, entering_ref, segments_ref, gain_ref, earlier_ref, key_ref,
    value_ref, query_ref, before_ref, cotangent_ref,
    attended_ref, own_ref, pieces_out,
    scale_ref, x_ref, normed_ref, pieces_ref, semaphores,
):
    (scale,) = begin([(scale_in, scale_ref)], semaphores)
    is_first = where_ref[0] == 0
    shard = own_ref.shape[1]
    cores, planes = received_ref.shape[:2]

    @pl.when(is_first)
    def _():
        x_ref[...] = entering_ref[...]

    @pl.when(jnp.logical_not(is_first))
    def _():
        for core in range(cores):
            for plane in range(planes):
                head = plane * cores + core
                x_ref[:, head * shard : (head + 1) * shard] = received_ref[core, plane]

    for head in range(cores * planes):

        @pl.when(where_ref[3] == head)
        def _():
            own_ref[...] = x_ref[:, head * shard : (head + 1) * shard]

    normalise(x_ref, root_mean_square(x_ref), gain_ref, normed_ref)
    gradient_pieces(before_ref, normed_ref, cotangent_ref, pieces_ref)
    pieces_copy = pltpu.make_async_copy(pieces_ref, pieces_out, semaphores.at[1])
    pieces_copy.start()
    scale.wait()
    row = segments_ref[pl.ds(where_ref[1], 1), :]
    ready = (lambda: None,) * 4
    attend(
        normed_ref, row, is_first, key_ref, value_ref, query_ref, scale_ref, blend_ref, earlier_ref, ready,
        attended_ref, None,
    )
    pieces_copy.wait()


def last_kernel(
    where_ref, near_ref, far_ref, weight_ref, own_ref, exchanged_in, out_ref, total_ref, exchanged_ref, semaphores
):
    (exchanged,) = begin([(exchanged_in, exchanged_ref)], semaphores)
    product = own_ref[...].astype(jnp.float32)
    cores, _, width = near_ref.shape
    for side_ref, plane in ((near_ref, where_ref[2]), (far_ref, 1 - where_ref[2])):
        for core in range(cores):
            start = pl.multiple_of((plane * cores + core) * width, width)
            product += jnp.dot(side_ref[core], weight_ref[pl.ds(start, width), :], preferred_element_type=jnp.float32)
    out_ref[...] = product.astype(jnp.bfloat16)
    exchanged.wait()
    total = exchanged_ref[0].astype(jnp.float32)
    for replica in range(1, exchanged_ref.shape[0]):
        total += exchanged_ref[replica].astype(jnp.float32)
    total_ref[...] = total.T


PARAMS = pltpu.CompilerParams(vmem_limit_bytes=16 * 1024 * 1024)


def per_device(
    segments,
    section_input_stream,
    entering,
    pending_first_values,
    norm_gain_vector,
    query_weight,
    key_weight,
    value_weight,
    output_weight,
    query_key_scale,
    value_blend_weight,
    value_cotangent_rows,
):
    section_index = lax.axis_index("section")
    head_index = lax.axis_index("head")
    is_first = section_index == 0
    width = output_weight.shape[1]
    shard_width = output_weight.shape[2]
    total_batches, tokens = segments.shape
    kv_width = key_weight.shape[2]
    replicas = lax.axis_size("dp")
    grad_rows = width // replicas
    query_proj = query_weight[0]
    key_proj = key_weight[0]
    value_proj = value_weight[0]
    out_proj = output_weight[0]
    q_width = query_proj.shape[1]
    shape = jax.ShapeDtypeStruct
    half, floats = jnp.bfloat16, jnp.float32
    slots = jnp.arange(4, dtype=jnp.int32)
    before = jnp.where(is_first, total_batches - 1, section_index - 1)
    plane = head_index // (lax.axis_size("head") // 2)
    where = jnp.where(
        slots < 2,
        jnp.where(slots == 0, section_index, before),
        jnp.where(slots == 2, plane, head_index),
    ).astype(jnp.int32)
    own_first = section_input_stream[0]

    def project(own_rows, attended):
        return (
            own_rows.astype(floats)
            + jnp.dot(collect(attended), out_proj, preferred_element_type=floats)
        ).astype(half)

    in_hbm = [
        pltpu.with_memory_space_constraint(array, pltpu.HBM)
        for array in (
            segments, norm_gain_vector, query_key_scale, pending_first_values[0], key_proj,
            value_proj, query_proj,
        )
    ]
    attended_first, carried_first, normed_first = pl.pallas_call(
        first_kernel,
        out_shape=(
            shape((tokens, q_width), half),
            shape((tokens, kv_width), half),
            shape((tokens, width), half),
        ),
        in_specs=[SMEM, SMEM, VMEM] + [HBM] * 7,
        out_specs=(VMEM, VMEM, HBM),
        scratch_shapes=[
            (pltpu.SMEM if array.size < LANES else pltpu.VMEM)(array.shape, array.dtype) for array in in_hbm
        ]
        + [pltpu.VMEM((tokens, width), half), pltpu.SemaphoreType.DMA((8,))],
        compiler_params=PARAMS,
        name="first_round",
    )(where, value_blend_weight, collect(own_first), *in_hbm)
    output_first = project(own_first, attended_first)
    received_half = next_section(collect_planes(output_first))
    received_values = next_section(carried_first)
    attended_second, own_second, pieces = pl.pallas_call(
        second_kernel,
        out_shape=(
            shape((tokens, q_width), half),
            shape((tokens, shard_width), half),
            shape((replicas, kv_width, grad_rows), half),
        ),
        in_specs=[SMEM, SMEM, HBM] + [VMEM] * 10,
        out_specs=(VMEM, VMEM, HBM),
        scratch_shapes=[
            pltpu.SMEM(query_key_scale.shape, floats),
            pltpu.VMEM((tokens, width), half),
            pltpu.VMEM((tokens, width), half),
            pltpu.VMEM((replicas, kv_width, grad_rows), half),
            pltpu.SemaphoreType.DMA((2,)),
        ],
        compiler_params=PARAMS,
        name="second_round",
    )(
        where, value_blend_weight, in_hbm[2], collect_chip(received_half), entering, segments, norm_gain_vector,
        received_values, key_proj, value_proj, query_proj, normed_first, value_cotangent_rows[0],
    )
    across = swap_planes(attended_second)
    near = collect_chip(attended_second)

    once = lax.optimization_barrier(jnp.int32(1))
    exchanged = lax.fori_loop(0, once, lambda _, sent: lax.all_to_all(sent, "dp", 0, 0, tiled=True), pieces)
    across, near, exchanged = lax.optimization_barrier((across, near, exchanged))
    far = collect_chip(across)
    output_second, gradients = pl.pallas_call(
        last_kernel,
        out_shape=(shape((tokens, shard_width), half), shape((grad_rows, kv_width), floats)),
        in_specs=[SMEM] + [VMEM] * 4 + [HBM],
        out_specs=(VMEM, VMEM),
        scratch_shapes=[pltpu.VMEM(exchanged.shape, half), pltpu.SemaphoreType.DMA((1,))],
        compiler_params=PARAMS,
        name="last",
    )(where, near, far, out_proj, own_second, pltpu.with_memory_space_constraint(exchanged, pltpu.HBM))
    return (output_first[None], output_second[None], gradients[None])


def solution(mesh):
    return jax.shard_map(
        per_device,
        mesh=mesh,
        in_specs=(
            P(None, "dp"),
            P("section", "dp", "head"),
            P("dp", None),
            P("section", "dp", "head"),
            P("section", None),
            P("section", None, "head"),
            P("section", None, "head"),
            P("section", None, "head"),
            P("section", None, "head"),
            P("section", "head"),
            P("section", "head"),
            P("section", None, "dp", "head"),
        ),
        out_specs=(
            P("section", "dp", "head"),
            P("section", "dp", "head"),
            P("section", "dp", "head"),
        ),
        check_vma=False,
    )
```

```python
import math

import jax
import jax.numpy as jnp
from jax import lax
from jax.experimental import pallas as pl
from jax.experimental.pallas import tpu as pltpu
from jax.sharding import PartitionSpec as P

HEAD_WIDTH = 128
EPSILON = 1e-06
LANES = 128

VMEM = pl.BlockSpec(memory_space=pltpu.VMEM)
SMEM = pl.BlockSpec(memory_space=pltpu.SMEM)
HBM = pl.BlockSpec(memory_space=pltpu.HBM)


def collect(piece):
    return lax.all_gather(piece, "head", axis=1, tiled=True)


def collect_chip(piece):
    peers = lax.axis_size("head")
    chips = [[i, i + 1] for i in range(0, peers, 2)]
    return lax.all_gather(piece, "head", axis_index_groups=chips)


def collect_planes(piece):
    peers = lax.axis_size("head")
    pairs = [[i, i + peers // 2] for i in range(peers // 2)]
    return lax.all_gather(piece, "head", axis_index_groups=pairs)


def swap_planes(piece):
    peers = lax.axis_size("head")
    return lax.ppermute(piece, "head", [(i, (i + peers // 2) % peers) for i in range(peers)])


def next_section(piece):
    peers = lax.axis_size("section")
    return lax.ppermute(piece, "section", [(i, i + 1) for i in range(peers - 1)])


def rms_rows(values):
    return values * lax.rsqrt(jnp.mean(values * values, axis=-1, keepdims=True) + EPSILON)


def begin(pairs, semaphores):
    copies = [pltpu.make_async_copy(src, dst, semaphores.at[i]) for i, (src, dst) in enumerate(pairs)]
    for copy in copies:
        copy.start()
    return copies


def root_mean_square(x_ref):
    tokens, width = x_ref.shape
    squares = jnp.zeros((tokens, LANES), jnp.float32)
    for start in range(0, width, LANES):
        part = x_ref[:, start : start + LANES].astype(jnp.float32)
        squares += part * part
    return lax.rsqrt(jnp.sum(squares, axis=-1, keepdims=True) / width + EPSILON)


def normalise(x_ref, root, gain_ref, normed_ref):
    for start in range(0, x_ref.shape[1], LANES):
        columns = slice(start, start + LANES)
        part = x_ref[:, columns].astype(jnp.float32)
        normed_ref[:, columns] = (part * root * gain_ref[:, columns]).astype(jnp.bfloat16)


def attend(
    normed_ref, row, is_first, key_ref, value_ref, query_ref, scale_ref, blend_ref, earlier_ref, waits, attended_ref,
    carried_ref,
):
    key_wait, value_wait, earlier_wait, query_wait = waits
    tokens = normed_ref.shape[0]
    local_heads = query_ref.shape[1] // HEAD_WIDTH
    across = jnp.broadcast_to(row, (tokens, tokens))
    down = across.T
    later = lax.broadcasted_iota(jnp.int32, (tokens, tokens), 0)
    sooner = lax.broadcasted_iota(jnp.int32, (tokens, tokens), 1)
    allowed = (later >= sooner) & (across == down)
    normed = normed_ref[...]
    key_wait()
    keys = rms_rows(jnp.dot(normed, key_ref[...], preferred_element_type=jnp.float32))
    value_wait()
    values = jnp.dot(normed, value_ref[...], preferred_element_type=jnp.float32)
    earlier_wait()
    own = values.astype(jnp.bfloat16)
    earlier = earlier_ref[...]
    blended = (values + blend_ref[0, 0] * earlier.astype(jnp.float32)).astype(jnp.bfloat16)
    mixed = jnp.where(is_first, own, blended)
    if carried_ref is not None:
        carried_ref[...] = jnp.where(is_first, own, earlier)
    query_wait()
    queries = jnp.dot(normed, query_ref[...], preferred_element_type=jnp.float32)
    for head in range(local_heads):
        columns = slice(head * HEAD_WIDTH, (head + 1) * HEAD_WIDTH)
        query = rms_rows(queries[:, columns])
        scores = lax.dot_general(
            query,
            keys,
            (((1,), (1,)), ((), ())),
            precision=lax.Precision.HIGHEST,
            preferred_element_type=jnp.float32,
        )
        scores = scores * (scale_ref[0, head] / math.sqrt(HEAD_WIDTH))
        scores = jnp.where(allowed, scores, -jnp.inf)
        exponent = jnp.exp(scores - jnp.max(scores, axis=-1, keepdims=True))
        weights = (exponent / jnp.sum(exponent, axis=-1, keepdims=True)).astype(jnp.bfloat16)
        attended_ref[:, columns] = jnp.dot(
            weights, mixed, preferred_element_type=jnp.float32
        ).astype(jnp.bfloat16)


def first_kernel(
    where_ref, blend_ref, x_ref, segments_in, gain_in, scale_in, earlier_in, key_in, value_in, query_in,
    attended_ref, carried_ref, normed_out,
    segments_ref, gain_ref, scale_ref, earlier_ref, key_ref, value_ref, query_ref, normed_ref, semaphores,
):
    gain, segments, scale, earlier, key, value, query = begin(
        [
            (gain_in, gain_ref),
            (segments_in, segments_ref),
            (scale_in, scale_ref),
            (earlier_in, earlier_ref),
            (key_in, key_ref),
            (value_in, value_ref),
            (query_in, query_ref),
        ],
        semaphores,
    )
    root = root_mean_square(x_ref)
    gain.wait()
    normalise(x_ref, root, gain_ref, normed_ref)
    normed_copy = pltpu.make_async_copy(normed_ref, normed_out, semaphores.at[7])
    normed_copy.start()
    segments.wait()
    scale.wait()
    row = segments_ref[pl.ds(where_ref[0], 1), :]
    attend(
        normed_ref, row, where_ref[0] == 0, key_ref, value_ref, query_ref, scale_ref, blend_ref, earlier_ref,
        (key.wait, value.wait, earlier.wait, query.wait), attended_ref, carried_ref,
    )
    normed_copy.wait()


def gradient_pieces(before_ref, normed_ref, cotangent_ref, pieces_ref):
    replicas = pieces_ref.shape[0]
    rows = normed_ref.shape[1] // replicas
    contract = (((1,), (0,)), ((), ()))
    first = cotangent_ref[0].astype(jnp.float32).T.astype(jnp.bfloat16)
    second = cotangent_ref[1].astype(jnp.float32).T.astype(jnp.bfloat16)
    for replica in range(replicas):
        columns = slice(replica * rows, (replica + 1) * rows)
        term = lax.dot_general(first, before_ref[:, columns], contract, preferred_element_type=jnp.float32)
        term += lax.dot_general(second, normed_ref[:, columns], contract, preferred_element_type=jnp.float32)
        pieces_ref[replica] = term.astype(jnp.bfloat16)


def second_kernel(
    where_ref, blend_ref, scale_in, received_ref, entering_ref, segments_ref, gain_ref, earlier_ref, key_ref,
    value_ref, query_ref, before_ref, cotangent_ref,
    attended_ref, own_ref, pieces_out,
    scale_ref, x_ref, normed_ref, pieces_ref, semaphores,
):
    (scale,) = begin([(scale_in, scale_ref)], semaphores)
    is_first = where_ref[0] == 0
    shard = own_ref.shape[1]
    cores, planes = received_ref.shape[:2]

    @pl.when(is_first)
    def _():
        x_ref[...] = entering_ref[...]

    @pl.when(jnp.logical_not(is_first))
    def _():
        for core in range(cores):
            for plane in range(planes):
                head = plane * cores + core
                x_ref[:, head * shard : (head + 1) * shard] = received_ref[core, plane]

    for head in range(cores * planes):

        @pl.when(where_ref[3] == head)
        def _():
            own_ref[...] = x_ref[:, head * shard : (head + 1) * shard]

    normalise(x_ref, root_mean_square(x_ref), gain_ref, normed_ref)
    gradient_pieces(before_ref, normed_ref, cotangent_ref, pieces_ref)
    pieces_copy = pltpu.make_async_copy(pieces_ref, pieces_out, semaphores.at[1])
    pieces_copy.start()
    scale.wait()
    row = segments_ref[pl.ds(where_ref[1], 1), :]
    ready = (lambda: None,) * 4
    attend(
        normed_ref, row, is_first, key_ref, value_ref, query_ref, scale_ref, blend_ref, earlier_ref, ready,
        attended_ref, None,
    )
    pieces_copy.wait()


def projected(heads_ref, plane, weight_ref):
    cores, tokens, width = heads_ref.shape
    product = jnp.zeros((tokens, weight_ref.shape[1]), jnp.float32)
    for core in range(cores):
        start = pl.multiple_of((plane * cores + core) * width, width)
        product += jnp.dot(heads_ref[core], weight_ref[pl.ds(start, width), :], preferred_element_type=jnp.float32)
    return product


def near_kernel(where_ref, near_ref, weight_ref, own_ref, exchanged_in, partial_ref, total_ref, exchanged_ref, semaphores):
    (exchanged,) = begin([(exchanged_in, exchanged_ref)], semaphores)
    partial_ref[...] = own_ref[...].astype(jnp.float32) + projected(near_ref, where_ref[2], weight_ref)
    exchanged.wait()
    total = exchanged_ref[0].astype(jnp.float32)
    for replica in range(1, exchanged_ref.shape[0]):
        total += exchanged_ref[replica].astype(jnp.float32)
    total_ref[...] = total.T


def last_kernel(where_ref, far_ref, weight_ref, partial_ref, out_ref):
    out_ref[...] = (partial_ref[...] + projected(far_ref, 1 - where_ref[2], weight_ref)).astype(jnp.bfloat16)


PARAMS = pltpu.CompilerParams(vmem_limit_bytes=16 * 1024 * 1024)


def per_device(
    segments,
    section_input_stream,
    entering,
    pending_first_values,
    norm_gain_vector,
    query_weight,
    key_weight,
    value_weight,
    output_weight,
    query_key_scale,
    value_blend_weight,
    value_cotangent_rows,
):
    section_index = lax.axis_index("section")
    head_index = lax.axis_index("head")
    is_first = section_index == 0
    width = output_weight.shape[1]
    shard_width = output_weight.shape[2]
    total_batches, tokens = segments.shape
    kv_width = key_weight.shape[2]
    replicas = lax.axis_size("dp")
    grad_rows = width // replicas
    query_proj = query_weight[0]
    key_proj = key_weight[0]
    value_proj = value_weight[0]
    out_proj = output_weight[0]
    q_width = query_proj.shape[1]
    shape = jax.ShapeDtypeStruct
    half, floats = jnp.bfloat16, jnp.float32
    slots = jnp.arange(4, dtype=jnp.int32)
    before = jnp.where(is_first, total_batches - 1, section_index - 1)
    plane = head_index // (lax.axis_size("head") // 2)
    where = jnp.where(
        slots < 2,
        jnp.where(slots == 0, section_index, before),
        jnp.where(slots == 2, plane, head_index),
    ).astype(jnp.int32)
    own_first = section_input_stream[0]

    def project(own_rows, attended):
        return (
            own_rows.astype(floats)
            + jnp.dot(collect(attended), out_proj, preferred_element_type=floats)
        ).astype(half)

    in_hbm = [
        pltpu.with_memory_space_constraint(array, pltpu.HBM)
        for array in (
            segments, norm_gain_vector, query_key_scale, pending_first_values[0], key_proj,
            value_proj, query_proj,
        )
    ]
    attended_first, carried_first, normed_first = pl.pallas_call(
        first_kernel,
        out_shape=(
            shape((tokens, q_width), half),
            shape((tokens, kv_width), half),
            shape((tokens, width), half),
        ),
        in_specs=[SMEM, SMEM, VMEM] + [HBM] * 7,
        out_specs=(VMEM, VMEM, HBM),
        scratch_shapes=[
            (pltpu.SMEM if array.size < LANES else pltpu.VMEM)(array.shape, array.dtype) for array in in_hbm
        ]
        + [pltpu.VMEM((tokens, width), half), pltpu.SemaphoreType.DMA((8,))],
        compiler_params=PARAMS,
        name="first_round",
    )(where, value_blend_weight, collect(own_first), *in_hbm)
    output_first = project(own_first, attended_first)
    received_half = next_section(collect_planes(output_first))
    received_values = next_section(carried_first)
    attended_second, own_second, pieces = pl.pallas_call(
        second_kernel,
        out_shape=(
            shape((tokens, q_width), half),
            shape((tokens, shard_width), half),
            shape((replicas, kv_width, grad_rows), half),
        ),
        in_specs=[SMEM, SMEM, HBM] + [VMEM] * 10,
        out_specs=(VMEM, VMEM, HBM),
        scratch_shapes=[
            pltpu.SMEM(query_key_scale.shape, floats),
            pltpu.VMEM((tokens, width), half),
            pltpu.VMEM((tokens, width), half),
            pltpu.VMEM((replicas, kv_width, grad_rows), half),
            pltpu.SemaphoreType.DMA((2,)),
        ],
        compiler_params=PARAMS,
        name="second_round",
    )(
        where, value_blend_weight, in_hbm[2], collect_chip(received_half), entering, segments, norm_gain_vector,
        received_values, key_proj, value_proj, query_proj, normed_first, value_cotangent_rows[0],
    )
    across = swap_planes(attended_second)
    near = collect_chip(attended_second)

    once = lax.optimization_barrier(jnp.int32(1))
    exchanged = lax.fori_loop(0, once, lambda _, sent: lax.all_to_all(sent, "dp", 0, 0, tiled=True), pieces)
    partial, gradients = pl.pallas_call(
        near_kernel,
        out_shape=(shape((tokens, shard_width), floats), shape((grad_rows, kv_width), floats)),
        in_specs=[SMEM] + [VMEM] * 3 + [HBM],
        out_specs=(VMEM, VMEM),
        scratch_shapes=[pltpu.VMEM(exchanged.shape, half), pltpu.SemaphoreType.DMA((1,))],
        compiler_params=PARAMS,
        name="near",
    )(where, near, out_proj, own_second, pltpu.with_memory_space_constraint(exchanged, pltpu.HBM))
    across, partial = lax.optimization_barrier((across, partial))
    output_second = pl.pallas_call(
        last_kernel,
        out_shape=shape((tokens, shard_width), half),
        in_specs=[SMEM] + [VMEM] * 3,
        out_specs=VMEM,
        compiler_params=PARAMS,
        name="last",
    )(where, collect_chip(across), out_proj, partial)
    return (output_first[None], output_second[None], gradients[None])


def solution(mesh):
    return jax.shard_map(
        per_device,
        mesh=mesh,
        in_specs=(
            P(None, "dp"),
            P("section", "dp", "head"),
            P("dp", None),
            P("section", "dp", "head"),
            P("section", None),
            P("section", None, "head"),
            P("section", None, "head"),
            P("section", None, "head"),
            P("section", None, "head"),
            P("section", "head"),
            P("section", "head"),
            P("section", None, "dp", "head"),
        ),
        out_specs=(
            P("section", "dp", "head"),
            P("section", "dp", "head"),
            P("section", "dp", "head"),
        ),
        check_vma=False,
    )
```

```python
import math

import jax
import jax.numpy as jnp
from jax import lax
from jax.experimental import pallas as pl
from jax.experimental.pallas import tpu as pltpu
from jax.sharding import PartitionSpec as P

HEAD_WIDTH = 128
EPSILON = 1e-06
LANES = 128

VMEM = pl.BlockSpec(memory_space=pltpu.VMEM)
SMEM = pl.BlockSpec(memory_space=pltpu.SMEM)
HBM = pl.BlockSpec(memory_space=pltpu.HBM)


def collect(piece):
    return lax.all_gather(piece, "head", axis=1, tiled=True)


def collect_chip(piece):
    peers = lax.axis_size("head")
    chips = [[i, i + 1] for i in range(0, peers, 2)]
    return lax.all_gather(piece, "head", axis_index_groups=chips)


def collect_planes(piece):
    peers = lax.axis_size("head")
    pairs = [[i, i + peers // 2] for i in range(peers // 2)]
    return lax.all_gather(piece, "head", axis_index_groups=pairs)


def swap_planes(piece):
    peers = lax.axis_size("head")
    return lax.ppermute(piece, "head", [(i, (i + peers // 2) % peers) for i in range(peers)])


def next_section(piece):
    peers = lax.axis_size("section")
    return lax.ppermute(piece, "section", [(i, i + 1) for i in range(peers - 1)])


def rms_rows(values):
    return values * lax.rsqrt(jnp.mean(values * values, axis=-1, keepdims=True) + EPSILON)


def begin(pairs, semaphores):
    copies = [pltpu.make_async_copy(src, dst, semaphores.at[i]) for i, (src, dst) in enumerate(pairs)]
    for copy in copies:
        copy.start()
    return copies


def root_mean_square(x_ref):
    tokens, width = x_ref.shape
    squares = jnp.zeros((tokens, LANES), jnp.float32)
    for start in range(0, width, LANES):
        part = x_ref[:, start : start + LANES].astype(jnp.float32)
        squares += part * part
    return lax.rsqrt(jnp.sum(squares, axis=-1, keepdims=True) / width + EPSILON)


def normalise(x_ref, root, gain_ref, normed_ref):
    for start in range(0, x_ref.shape[1], LANES):
        columns = slice(start, start + LANES)
        part = x_ref[:, columns].astype(jnp.float32)
        normed_ref[:, columns] = (part * root * gain_ref[:, columns]).astype(jnp.bfloat16)


def attend(
    normed_ref, row, is_first, key_ref, value_ref, query_ref, scale_ref, blend_ref, earlier_ref, waits, attended_ref,
    carried_ref,
):
    key_wait, value_wait, earlier_wait, query_wait = waits
    tokens = normed_ref.shape[0]
    local_heads = query_ref.shape[1] // HEAD_WIDTH
    across = jnp.broadcast_to(row, (tokens, tokens))
    down = across.T
    later = lax.broadcasted_iota(jnp.int32, (tokens, tokens), 0)
    sooner = lax.broadcasted_iota(jnp.int32, (tokens, tokens), 1)
    allowed = (later >= sooner) & (across == down)
    normed = normed_ref[...]
    key_wait()
    keys = rms_rows(jnp.dot(normed, key_ref[...], preferred_element_type=jnp.float32))
    value_wait()
    values = jnp.dot(normed, value_ref[...], preferred_element_type=jnp.float32)
    earlier_wait()
    own = values.astype(jnp.bfloat16)
    earlier = earlier_ref[...]
    blended = (values + blend_ref[0, 0] * earlier.astype(jnp.float32)).astype(jnp.bfloat16)
    mixed = jnp.where(is_first, own, blended)
    if carried_ref is not None:
        carried_ref[...] = jnp.where(is_first, own, earlier)
    query_wait()
    queries = jnp.dot(normed, query_ref[...], preferred_element_type=jnp.float32)
    stacked = rms_rows(
        jnp.concatenate([queries[:, h * HEAD_WIDTH : (h + 1) * HEAD_WIDTH] for h in range(local_heads)])
    )
    products = lax.dot_general(
        stacked,
        keys,
        (((1,), (1,)), ((), ())),
        precision=lax.Precision.HIGHEST,
        preferred_element_type=jnp.float32,
    )
    weights = []
    for head in range(local_heads):
        scores = products[head * tokens : (head + 1) * tokens] * (scale_ref[0, head] / math.sqrt(HEAD_WIDTH))
        scores = jnp.where(allowed, scores, -jnp.inf)
        exponent = jnp.exp(scores - jnp.max(scores, axis=-1, keepdims=True))
        weights.append((exponent / jnp.sum(exponent, axis=-1, keepdims=True)).astype(jnp.bfloat16))
    attended = jnp.dot(jnp.concatenate(weights), mixed, preferred_element_type=jnp.float32)
    for head in range(local_heads):
        columns = slice(head * HEAD_WIDTH, (head + 1) * HEAD_WIDTH)
        attended_ref[:, columns] = attended[head * tokens : (head + 1) * tokens].astype(jnp.bfloat16)


def first_kernel(
    where_ref, blend_ref, x_ref, segments_in, gain_in, scale_in, earlier_in, key_in, value_in, query_in,
    attended_ref, carried_ref, normed_out,
    segments_ref, gain_ref, scale_ref, earlier_ref, key_ref, value_ref, query_ref, normed_ref, semaphores,
):
    gain, segments, scale, earlier, key, value, query = begin(
        [
            (gain_in, gain_ref),
            (segments_in, segments_ref),
            (scale_in, scale_ref),
            (earlier_in, earlier_ref),
            (key_in, key_ref),
            (value_in, value_ref),
            (query_in, query_ref),
        ],
        semaphores,
    )
    root = root_mean_square(x_ref)
    gain.wait()
    normalise(x_ref, root, gain_ref, normed_ref)
    normed_copy = pltpu.make_async_copy(normed_ref, normed_out, semaphores.at[7])
    normed_copy.start()
    segments.wait()
    scale.wait()
    row = segments_ref[pl.ds(where_ref[0], 1), :]
    attend(
        normed_ref, row, where_ref[0] == 0, key_ref, value_ref, query_ref, scale_ref, blend_ref, earlier_ref,
        (key.wait, value.wait, earlier.wait, query.wait), attended_ref, carried_ref,
    )
    normed_copy.wait()


def gradient_pieces(before_ref, normed_ref, cotangent_ref, pieces_ref):
    replicas = pieces_ref.shape[0]
    rows = normed_ref.shape[1] // replicas
    contract = (((1,), (0,)), ((), ()))
    first = cotangent_ref[0].astype(jnp.float32).T.astype(jnp.bfloat16)
    second = cotangent_ref[1].astype(jnp.float32).T.astype(jnp.bfloat16)
    for replica in range(replicas):
        columns = slice(replica * rows, (replica + 1) * rows)
        term = lax.dot_general(first, before_ref[:, columns], contract, preferred_element_type=jnp.float32)
        term += lax.dot_general(second, normed_ref[:, columns], contract, preferred_element_type=jnp.float32)
        pieces_ref[replica] = term.astype(jnp.bfloat16)


def second_kernel(
    where_ref, blend_ref, scale_in, received_ref, entering_ref, segments_ref, gain_ref, earlier_ref, key_ref,
    value_ref, query_ref, before_ref, cotangent_ref,
    attended_ref, own_ref, pieces_out,
    scale_ref, x_ref, normed_ref, pieces_ref, semaphores,
):
    (scale,) = begin([(scale_in, scale_ref)], semaphores)
    is_first = where_ref[0] == 0
    shard = own_ref.shape[1]
    cores, planes = received_ref.shape[:2]

    @pl.when(is_first)
    def _():
        x_ref[...] = entering_ref[...]

    @pl.when(jnp.logical_not(is_first))
    def _():
        for core in range(cores):
            for plane in range(planes):
                head = plane * cores + core
                x_ref[:, head * shard : (head + 1) * shard] = received_ref[core, plane]

    for head in range(cores * planes):

        @pl.when(where_ref[3] == head)
        def _():
            own_ref[...] = x_ref[:, head * shard : (head + 1) * shard]

    normalise(x_ref, root_mean_square(x_ref), gain_ref, normed_ref)
    gradient_pieces(before_ref, normed_ref, cotangent_ref, pieces_ref)
    pieces_copy = pltpu.make_async_copy(pieces_ref, pieces_out, semaphores.at[1])
    pieces_copy.start()
    scale.wait()
    row = segments_ref[pl.ds(where_ref[1], 1), :]
    ready = (lambda: None,) * 4
    attend(
        normed_ref, row, is_first, key_ref, value_ref, query_ref, scale_ref, blend_ref, earlier_ref, ready,
        attended_ref, None,
    )
    pieces_copy.wait()


def projected(heads_ref, plane, weight_ref):
    cores, tokens, width = heads_ref.shape
    product = jnp.zeros((tokens, weight_ref.shape[1]), jnp.float32)
    for core in range(cores):
        start = pl.multiple_of((plane * cores + core) * width, width)
        product += jnp.dot(heads_ref[core], weight_ref[pl.ds(start, width), :], preferred_element_type=jnp.float32)
    return product


def near_kernel(where_ref, near_ref, weight_ref, own_ref, exchanged_in, partial_ref, total_ref, exchanged_ref, semaphores):
    (exchanged,) = begin([(exchanged_in, exchanged_ref)], semaphores)
    partial_ref[...] = own_ref[...].astype(jnp.float32) + projected(near_ref, where_ref[2], weight_ref)
    exchanged.wait()
    total = exchanged_ref[0].astype(jnp.float32)
    for replica in range(1, exchanged_ref.shape[0]):
        total += exchanged_ref[replica].astype(jnp.float32)
    total_ref[...] = total.T


def last_kernel(where_ref, far_ref, weight_ref, partial_ref, out_ref):
    out_ref[...] = (partial_ref[...] + projected(far_ref, 1 - where_ref[2], weight_ref)).astype(jnp.bfloat16)


PARAMS = pltpu.CompilerParams(vmem_limit_bytes=16 * 1024 * 1024)


def per_device(
    segments,
    section_input_stream,
    entering,
    pending_first_values,
    norm_gain_vector,
    query_weight,
    key_weight,
    value_weight,
    output_weight,
    query_key_scale,
    value_blend_weight,
    value_cotangent_rows,
):
    section_index = lax.axis_index("section")
    head_index = lax.axis_index("head")
    is_first = section_index == 0
    width = output_weight.shape[1]
    shard_width = output_weight.shape[2]
    total_batches, tokens = segments.shape
    kv_width = key_weight.shape[2]
    replicas = lax.axis_size("dp")
    grad_rows = width // replicas
    query_proj = query_weight[0]
    key_proj = key_weight[0]
    value_proj = value_weight[0]
    out_proj = output_weight[0]
    q_width = query_proj.shape[1]
    shape = jax.ShapeDtypeStruct
    half, floats = jnp.bfloat16, jnp.float32
    slots = jnp.arange(4, dtype=jnp.int32)
    before = jnp.where(is_first, total_batches - 1, section_index - 1)
    plane = head_index // (lax.axis_size("head") // 2)
    where = jnp.where(
        slots < 2,
        jnp.where(slots == 0, section_index, before),
        jnp.where(slots == 2, plane, head_index),
    ).astype(jnp.int32)
    own_first = section_input_stream[0]

    def project(own_rows, attended):
        return (
            own_rows.astype(floats)
            + jnp.dot(collect(attended), out_proj, preferred_element_type=floats)
        ).astype(half)

    in_hbm = [
        pltpu.with_memory_space_constraint(array, pltpu.HBM)
        for array in (
            segments, norm_gain_vector, query_key_scale, pending_first_values[0], key_proj,
            value_proj, query_proj,
        )
    ]
    attended_first, carried_first, normed_first = pl.pallas_call(
        first_kernel,
        out_shape=(
            shape((tokens, q_width), half),
            shape((tokens, kv_width), half),
            shape((tokens, width), half),
        ),
        in_specs=[SMEM, SMEM, VMEM] + [HBM] * 7,
        out_specs=(VMEM, VMEM, HBM),
        scratch_shapes=[
            (pltpu.SMEM if array.size < LANES else pltpu.VMEM)(array.shape, array.dtype) for array in in_hbm
        ]
        + [pltpu.VMEM((tokens, width), half), pltpu.SemaphoreType.DMA((8,))],
        compiler_params=PARAMS,
        name="first_round",
    )(where, value_blend_weight, collect(own_first), *in_hbm)
    output_first = project(own_first, attended_first)
    received_half = next_section(collect_planes(output_first))
    received_values = next_section(carried_first)
    attended_second, own_second, pieces = pl.pallas_call(
        second_kernel,
        out_shape=(
            shape((tokens, q_width), half),
            shape((tokens, shard_width), half),
            shape((replicas, kv_width, grad_rows), half),
        ),
        in_specs=[SMEM, SMEM, HBM] + [VMEM] * 10,
        out_specs=(VMEM, VMEM, HBM),
        scratch_shapes=[
            pltpu.SMEM(query_key_scale.shape, floats),
            pltpu.VMEM((tokens, width), half),
            pltpu.VMEM((tokens, width), half),
            pltpu.VMEM((replicas, kv_width, grad_rows), half),
            pltpu.SemaphoreType.DMA((2,)),
        ],
        compiler_params=PARAMS,
        name="second_round",
    )(
        where, value_blend_weight, in_hbm[2], collect_chip(received_half), entering, segments, norm_gain_vector,
        received_values, key_proj, value_proj, query_proj, normed_first, value_cotangent_rows[0],
    )
    across = swap_planes(attended_second)
    near = collect_chip(attended_second)

    once = lax.optimization_barrier(jnp.int32(1))
    exchanged = lax.fori_loop(0, once, lambda _, sent: lax.all_to_all(sent, "dp", 0, 0, tiled=True), pieces)
    partial, gradients = pl.pallas_call(
        near_kernel,
        out_shape=(shape((tokens, shard_width), floats), shape((grad_rows, kv_width), floats)),
        in_specs=[SMEM] + [VMEM] * 3 + [HBM],
        out_specs=(VMEM, VMEM),
        scratch_shapes=[pltpu.VMEM(exchanged.shape, half), pltpu.SemaphoreType.DMA((1,))],
        compiler_params=PARAMS,
        name="near",
    )(where, near, out_proj, own_second, pltpu.with_memory_space_constraint(exchanged, pltpu.HBM))
    across, partial = lax.optimization_barrier((across, partial))
    output_second = pl.pallas_call(
        last_kernel,
        out_shape=shape((tokens, shard_width), half),
        in_specs=[SMEM] + [VMEM] * 3,
        out_specs=VMEM,
        compiler_params=PARAMS,
        name="last",
    )(where, collect_chip(across), out_proj, partial)
    return (output_first[None], output_second[None], gradients[None])


def solution(mesh):
    return jax.shard_map(
        per_device,
        mesh=mesh,
        in_specs=(
            P(None, "dp"),
            P("section", "dp", "head"),
            P("dp", None),
            P("section", "dp", "head"),
            P("section", None),
            P("section", None, "head"),
            P("section", None, "head"),
            P("section", None, "head"),
            P("section", None, "head"),
            P("section", "head"),
            P("section", "head"),
            P("section", None, "dp", "head"),
        ),
        out_specs=(
            P("section", "dp", "head"),
            P("section", "dp", "head"),
            P("section", "dp", "head"),
        ),
        check_vma=False,
    )
```
